32 devices in a mesh: groups: 2 (over y), freq: 4 (over z), space: 2 (over x), blk: 2 (over core).
Axes of the slice: x: 2, y: 2, z: 4, core: 2. Of those that a mesh axis runs over, the one named last changes fastest.
Arguments:
- realizations: bfloat16 [16, 64, 2, 8192], P('freq', 'groups', None, ('space', 'blk')), parts along dimension 1, may hold values from -6 to 6
- weights: float32 [16384], P(('groups', 'space', 'blk')), parts along dimension 0, may hold values from 0.25 to 4
- partners: int32 [3, 4], replicated, may hold values from 0 to 3, each once within a row
- block_count: int32 [2], P('groups'), parts along dimension 0, may hold values from 16 to 32
Outputs:
- modes: bfloat16 [16, 64, 2, 8192], P('freq', 'groups', None, ('space', 'blk')), parts along dimension 1
- gram: float32 [6, 16, 4, 2, 32, 32], P('groups', 'freq'), parts along dimension 0
The draws below stay inside these ranges and needn't reach their ends.
There are 2 independent parts, one for each index of `groups`. The reference program is written for one: setup_inputs(seed, part) draws one part's arguments, and reference() takes and returns one part's arrays. A program takes and returns all parts, laid end to end along the dimension named above; an argument that names none is the same for every part. Nothing has to cross between parts.
Inputs may be any that keep to these rules, and one draw needn't show every extreme that they name: `partners`: each row is a permutation of the groups 0 to 3. `block_count`: blocks from this index on are left out.
All inputs are finite; a program needn't handle non-finite values.
Results may differ from the reference program's by a relative error of at most 0.0057.
Values may be sent and summed in bfloat16 or wider, within the bound.
A program may use at most 128 MiB of HBM per device.

```python
import math
import jax
import jax.numpy as jnp
from jax import lax

FREQ_DEV = 4
NB = 32
ROUNDS = 3
FREQ_SHARDS = 4
FREQS = 16
SPACE = 8192


def block_levels(own_key, shape, split, smallest, top_value):
    level, own = 1.0, jax.random.fold_in(own_key, 6)
    for position, shards_of in split:
        steps = jnp.exp(jax.random.uniform(jax.random.fold_in(own, position), (shards_of,), jnp.float32, smallest / len(split), top_value / len(split)))
        level = level * jnp.repeat(steps, shape[position] // shards_of).reshape([-1 if axis == position else 1 for axis in range(len(shape))])
    return level


def gaussian(rng, shape, scale, reach, pieces=(), held_as=jnp.bfloat16):
    values = scale * jax.random.normal(rng, shape, jnp.float32)
    if pieces:
        values = values * block_levels(rng, shape, pieces, -0.22, 0.18)
    return jnp.clip(values, -reach, reach).astype(held_as)


def setup_inputs(seed: int = 0, part: int = 0) -> dict:
    key_list = jax.random.split(jax.random.key(seed), 5)
    part_keys = jax.random.split(jax.random.fold_in(key_list[4], part), 5)
    realizations = gaussian(part_keys[0], (FREQS, NB, 2, SPACE), 1.0, 6.0, ((0, 4), (3, 4)))
    weights = jnp.clip(jnp.exp(math.log(4.0) - 2.7725887 * jax.random.uniform(part_keys[1], (SPACE,), jnp.float32) ** block_levels(part_keys[1], (SPACE,), ((0, 4),), -0.2, 0.2)), 0.25, 4.0)
    partners = jax.vmap(lambda own: jax.random.permutation(own, FREQ_SHARDS))(jax.random.split(key_list[2], ROUNDS)).reshape((ROUNDS, FREQ_SHARDS)).astype(jnp.int32)
    block_count = jax.random.randint(part_keys[3], (1,), NB // 2, NB + 1).astype(jnp.int32)
    return {"realizations": realizations, "weights": weights, "partners": partners, "block_count": block_count}


def triad_product(own_part, partner_part, point_weights):
    first = own_part[None]
    second = partner_part
    real_part = first[:, :, 0] * second[:, :, 0] - first[:, :, 1] * second[:, :, 1]
    imag_part = first[:, :, 0] * second[:, :, 1] + first[:, :, 1] * second[:, :, 0]
    return jnp.stack([real_part, imag_part], axis=2) * point_weights

def reference(realizations, weights, partners, block_count):
    keeper = (jnp.arange(NB, dtype=jnp.int32) < block_count[0]).astype(jnp.bfloat16)
    fields = realizations * keeper[None, :, None, None]
    gram_scale = 1.0 / jnp.sqrt(jnp.float32(SPACE))
    mode_scale = 1.0 / jnp.sqrt(jnp.float32(ROUNDS * FREQ_DEV * NB))
    offsets = jnp.arange(FREQ_DEV, dtype=jnp.int32)

    def single(freq_index):
        own_part = fields[freq_index].astype(jnp.float32)
        grams = []
        accumulated = jnp.zeros((NB, 2, SPACE), jnp.float32)
        for which_round in range(ROUNDS):
            partner_idx = partners[which_round, freq_index // FREQ_DEV] * FREQ_DEV + offsets
            target_idx = ((freq_index + partner_idx) % FREQS).astype(jnp.int32)
            partner_part = fields[partner_idx].astype(jnp.float32)
            targets = fields[target_idx].astype(jnp.float32)
            product = triad_product(own_part, partner_part, point_weights=weights).astype(jnp.bfloat16)
            product = lax.optimization_barrier(product).astype(jnp.float32)
            real_gram = jnp.einsum('jas,jbs->jab', product[:, :, 0], targets[:, :, 0]) + jnp.einsum('jas,jbs->jab', product[:, :, 1], targets[:, :, 1])
            imag_gram = jnp.einsum('jas,jbs->jab', product[:, :, 0], targets[:, :, 1]) - jnp.einsum('jas,jbs->jab', product[:, :, 1], targets[:, :, 0])
            gram_now = jnp.stack([real_gram, imag_gram], axis=1) * gram_scale
            grams.append(gram_now)
            rounded = lax.optimization_barrier(gram_now.astype(jnp.bfloat16)).astype(jnp.float32)
            real_mode = jnp.einsum('jab,jbs->as', rounded[:, 0], targets[:, :, 0]) - jnp.einsum('jab,jbs->as', rounded[:, 1], targets[:, :, 1])
            imag_mode = jnp.einsum('jab,jbs->as', rounded[:, 0], targets[:, :, 1]) + jnp.einsum('jab,jbs->as', rounded[:, 1], targets[:, :, 0])
            accumulated = accumulated + jnp.stack([real_mode, imag_mode], axis=1)
        return (jnp.stack(grams, axis=0), (accumulated * mode_scale).astype(jnp.bfloat16))
    all_grams, modes = lax.map(single, jnp.arange(FREQS, dtype=jnp.int32))
    gram = jnp.transpose(all_grams, (1, 0, 2, 3, 4, 5))
    return (modes, gram)
```

```python
import functools
import math

import jax
import jax.numpy as jnp
from jax import lax
from jax.experimental import pallas as pl
from jax.experimental.pallas import tpu as pltpu
from jax.sharding import PartitionSpec as P

MESH = pl.DeviceIdType.MESH
F32 = jnp.float32
BF16 = jnp.bfloat16
AXES = ("freq", "space", "blk")


def kernel(dims, partners_ref, x_ref, w_ref, out_ref, gram_ref,
           q, wq, sec, prod, gf, r1, b2, r2, b3, r3, gfull, mo,
           own_sem, in_s, in_r, c_s, c_r, x_s, x_r, z_s, z_r,
           gz_s, gz_r, gx_s, gx_r, gc_s, gc_r, out_s, out_r):
    nz, nx, nc, rounds, per, nb, pts, gram_scale, mode_scale = dims
    width = per * nb
    rows = per * 2 * nb
    half = rows // nc
    part = half // nx
    freqs = nz * per
    z = lax.axis_index("freq")
    x = lax.axis_index("space")
    c = lax.axis_index("blk")

    def peer(me, d, n):
        return lax.rem(me + d, n)

    barrier = pltpu.get_barrier_semaphore()
    for name, me, n in (("freq", z, nz), ("space", x, nx), ("blk", c, nc)):
        for d in range(1, n):
            pl.semaphore_signal(barrier, inc=1, device_id={name: peer(me, d, n)}, device_id_type=MESH)
    pl.semaphore_wait(barrier, nz + nx + nc - 3)

    def remote(src, dst, send, recv, name, to):
        copy = pltpu.make_async_remote_copy(
            src_ref=src, dst_ref=dst, send_sem=send, recv_sem=recv,
            device_id={name: to}, device_id_type=MESH)
        copy.start()
        return copy

    incoming = []
    mine = pl.ds(z * per, per)
    for d in range(nz - 1, 0, -1):
        to = peer(z, d, nz)
        incoming.append(remote(x_ref.at[to], q.at[:, mine], in_s.at[d], in_r.at[d], "freq", to))
    own = pltpu.make_async_copy(x_ref.at[z], q.at[:, mine], own_sem)
    own.start()
    own.wait()
    for copy in incoming:
        copy.wait_recv()

    weights = w_ref[pl.ds(z, 1), :]

    def weigh(f, carry):
        wq[0, f] = q[0, f].astype(F32) * weights
        wq[1, f] = q[1, f].astype(F32) * weights
        return carry

    lax.fori_loop(0, freqs, weigh, 0)

    lane_j = lax.broadcasted_iota(jnp.int32, (nb, width), 1) // nb

    def targets(g, p, i):
        at = [lax.rem((g + p) * per + i + j, freqs) for j in range(per)]
        return jnp.concatenate([q[h, t] for h in range(2) for t in at], axis=0)

    def grams(r):
        def group(g, carry):
            p = partners_ref[r, g]
            for h in range(2):
                for j in range(per):
                    sec[h, j] = q[h, p * per + j].astype(F32)

            def one(i, inner):
                first_re = wq[0, g * per + i]
                first_im = wq[1, g * per + i]
                for j in range(per):
                    second_re = sec[0, j]
                    second_im = sec[1, j]
                    prod[pl.ds(j * nb, nb), :] = (first_re * second_re - first_im * second_im).astype(BF16)
                    prod[pl.ds(width + j * nb, nb), :] = (first_re * second_im + first_im * second_re).astype(BF16)
                full = lax.dot_general(prod[...], targets(g, p, i), (((1,), (1,)), ((), ())),
                                       preferred_element_type=F32)
                g_re = full[:width, :width] + full[width:, width:]
                g_im = full[:width, width:] - full[width:, :width]
                re, im = g_re[:nb], g_im[:nb]
                for j in range(1, per):
                    keep = lane_j == j
                    re = jnp.where(keep, g_re[j * nb:(j + 1) * nb], re)
                    im = jnp.where(keep, g_im[j * nb:(j + 1) * nb], im)
                base = pl.multiple_of(i * 2 * nb, 2 * nb)
                gf[r, g, pl.ds(base, 2 * nb), :] = jnp.concatenate([re, im], axis=0)
                return inner

            return lax.fori_loop(0, per, one, carry)

        lax.fori_loop(0, nz, group, 0)

    half_at = pl.ds(pl.multiple_of(c * half, half), half)
    part_at = pl.ds(pl.multiple_of(c * half + x * part, part), part)
    in_half = pl.ds(pl.multiple_of(x * part, part), part)
    flight = {}
    sent = []

    def await_all(r, stage):
        for copy in flight[r, stage]:
            copy.wait_recv()
        sent.extend(flight[r, stage])

    def stage_run(r, stage):
        out = []
        if stage == 0:
            grams(r)
            for d in range(1, nc):
                to = peer(c, d, nc)
                at = pl.ds(pl.multiple_of(to * half, half), half)
                out.append(remote(gf.at[r, :, at, :], r1.at[r, d - 1], c_s.at[r, d], c_r.at[r, d], "blk", to))
        elif stage == 1:
            await_all(r, 0)
            total = gf[r, :, half_at, :]
            for d in range(1, nc):
                total = total + r1[r, d - 1]
            b2[r] = total.astype(BF16)
            gf[r, :, half_at, :] = total
            for d in range(1, nx):
                to = peer(x, d, nx)
                at = pl.ds(pl.multiple_of(to * part, part), part)
                out.append(remote(b2.at[r, :, at, :], r2.at[r, d - 1], x_s.at[r, d], x_r.at[r, d], "space", to))
        elif stage == 2:
            await_all(r, 1)
            total = gf[r, :, part_at, :]
            for d in range(1, nx):
                total = total + r2[r, d - 1].astype(F32)
            b3[r] = total.astype(BF16)
            gf[r, :, part_at, :] = total
            for d in range(nz - 1, 0, -1):
                to = peer(z, d, nz)
                out.append(remote(b3.at[r, to], r3.at[r, d - 1], z_s.at[r, d], z_r.at[r, d], "freq", to))
        elif stage == 3:
            await_all(r, 2)
            total = gf[r, z, part_at, :]
            for d in range(1, nz):
                total = total + r3[r, d - 1].astype(F32)
            gfull[r, z, part_at, :] = (total * gram_scale).astype(BF16)
            block = gfull.at[r, z, part_at, :]
            for d in range(nz - 1, 0, -1):
                to = peer(z, d, nz)
                out.append(remote(block, block, gz_s.at[r, d], gz_r.at[r, d], "freq", to))
        elif stage == 4:
            await_all(r, 3)
            block = gfull.at[r, :, part_at, :]
            for d in range(1, nx):
                out.append(remote(block, block, gx_s.at[r, d], gx_r.at[r, d], "space", peer(x, d, nx)))
        elif stage == 5:
            await_all(r, 4)
            block = gfull.at[r, :, half_at, :]
            for d in range(1, nc):
                out.append(remote(block, block, gc_s.at[r, d], gc_r.at[r, d], "blk", peer(c, d, nc)))
        else:
            await_all(r, 5)
            gram_ref[r] = gfull[r, z].astype(F32)
        flight[r, stage] = out

    for tick in range(7 + rounds - 1):
        for r in range(rounds):
            if 0 <= tick - r < 7:
                stage_run(r, tick - r)

    def modes(zk):
        def one(i, carry):
            total = None
            at = pl.multiple_of(i * 2 * nb, 2 * nb)
            for r in range(rounds):
                p = partners_ref[r, zk]
                re = gfull[r, zk, pl.ds(at, nb), :]
                im = gfull[r, zk, pl.ds(at + nb, nb), :]
                left = jnp.concatenate([jnp.concatenate([re, -im], axis=1),
                                        jnp.concatenate([im, re], axis=1)], axis=0)
                term = jnp.dot(left, targets(zk, p, i), preferred_element_type=F32)
                total = term if total is None else total + term
            mo[zk, pl.ds(at, 2 * nb), :] = (total * mode_scale).astype(BF16)
            return carry

        lax.fori_loop(0, per, one, 0)

    outgoing = []
    for d in range(nz - 1, 0, -1):
        to = peer(z, d, nz)
        modes(to)
        outgoing.append(remote(mo.at[to], out_ref.at[z], out_s.at[d], out_r.at[d], "freq", to))
    modes(z)
    keep = pltpu.make_async_copy(mo.at[z], out_ref.at[z], own_sem)
    keep.start()
    keep.wait()
    for copy in outgoing:
        copy.wait_recv()
    for copy in incoming + sent + outgoing:
        copy.wait_send()


def body(sizes, realizations, weights, partners, block_count):
    nz, nx, nc = sizes
    per, nb, _, points = realizations.shape
    rounds = partners.shape[0]
    pts = points // nz
    keeper = (jnp.arange(nb, dtype=jnp.int32) < block_count[0]).astype(BF16)
    fields = realizations * keeper[None, :, None, None]
    fields = fields.reshape(per, nb, 2, nz, pts).transpose(3, 2, 0, 1, 4)
    width = per * nb
    rows = 2 * per * nb
    half = rows // nc
    part = half // nx
    freqs = nz * per
    dims = (nz, nx, nc, rounds, per, nb, pts,
            1.0 / math.sqrt(points * nx * nc), 1.0 / math.sqrt(rounds * per * nb))
    dma = pltpu.SemaphoreType.DMA
    vmem = pl.BlockSpec(memory_space=pltpu.VMEM)
    modes, grams = pl.pallas_call(
        functools.partial(kernel, dims),
        out_shape=(jax.ShapeDtypeStruct((nz, rows, pts), BF16),
                   jax.ShapeDtypeStruct((rounds, rows, width), F32)),
        in_specs=[pl.BlockSpec(memory_space=pltpu.SMEM), vmem, vmem],
        out_specs=(vmem, vmem),
        scratch_shapes=[
            pltpu.VMEM((2, freqs, nb, pts), BF16),
            pltpu.VMEM((2, freqs, nb, pts), F32),
            pltpu.VMEM((2, per, nb, pts), F32),
            pltpu.VMEM((2 * width, pts), BF16),
            pltpu.VMEM((rounds, nz, rows, width), F32),
            pltpu.VMEM((rounds, nc - 1, nz, half, width), F32),
            pltpu.VMEM((rounds, nz, half, width), BF16),
            pltpu.VMEM((rounds, nx - 1, nz, part, width), BF16),
            pltpu.VMEM((rounds, nz, part, width), BF16),
            pltpu.VMEM((rounds, nz - 1, part, width), BF16),
            pltpu.VMEM((rounds, nz, rows, width), BF16),
            pltpu.VMEM((nz, rows, pts), BF16),
            dma,
            dma((nz,)), dma((nz,)),
            dma((rounds, nc)), dma((rounds, nc)),
            dma((rounds, nx)), dma((rounds, nx)),
            dma((rounds, nz)), dma((rounds, nz)),
            dma((rounds, nz)), dma((rounds, nz)),
            dma((rounds, nx)), dma((rounds, nx)),
            dma((rounds, nc)), dma((rounds, nc)),
            dma((nz,)), dma((nz,)),
        ],
        compiler_params=pltpu.CompilerParams(
            collective_id=0, has_side_effects=True, vmem_limit_bytes=56 * 1024 * 1024),
    )(partners, fields, weights.reshape(nz, pts))
    modes = modes.reshape(nz, per, 2, nb, pts).transpose(1, 3, 2, 0, 4).reshape(per, nb, 2, points)
    grams = grams.reshape(rounds, per, 2, nb, per, nb).transpose(0, 1, 4, 2, 3, 5)
    return (modes, grams)


def solution(mesh):
    placed = (
        P("freq", "groups", None, ("space", "blk")),
        P(("groups", "space", "blk")),
        P(),
        P("groups"),
    )
    return jax.shard_map(
        functools.partial(body, tuple(mesh.shape[a] for a in AXES)),
        mesh=mesh,
        in_specs=placed,
        out_specs=(
            P("freq", "groups", None, ("space", "blk")),
            P("groups", "freq", None, None, None, None),
        ),
        check_vma=False,
    )
```

```python
import functools
import math

import jax
import jax.numpy as jnp
from jax import lax
from jax.experimental import pallas as pl
from jax.experimental.pallas import tpu as pltpu
from jax.sharding import PartitionSpec as P

MESH = pl.DeviceIdType.MESH
F32 = jnp.float32
BF16 = jnp.bfloat16
AXES = ("freq", "space", "blk")


def kernel(dims, partners_ref, count_ref, x_ref, w_ref, out_ref, gram_ref,
           q, qf, wq, prod, gf, r1, b2, r2, b3, r3, gfull, mo,
           own_sem, in_s, in_r, c_s, c_r, x_s, x_r, z_s, z_r,
           gz_s, gz_r, gx_s, gx_r, gc_s, gc_r, out_s, out_r):
    nz, nx, nc, rounds, per, nb, pts, halves, chunks, gram_scale, mode_scale = dims
    width = per * nb
    each = per // chunks
    rows = each * 2 * nb
    half = rows // nc
    part = half // nx
    freqs = nz * per
    z = lax.axis_index("freq")
    x = lax.axis_index("space")
    c = lax.axis_index("blk")

    def peer(me, d, n):
        return lax.rem(me + d, n)

    barrier = pltpu.get_barrier_semaphore()
    for name, me, n in (("freq", z, nz), ("space", x, nx), ("blk", c, nc)):
        for d in range(1, n):
            pl.semaphore_signal(barrier, inc=1, device_id={name: peer(me, d, n)}, device_id_type=MESH)
    pl.semaphore_wait(barrier, nz + nx + nc - 3)

    def remote(src, dst, send, recv, name, to):
        copy = pltpu.make_async_remote_copy(
            src_ref=src, dst_ref=dst, send_sem=send, recv_sem=recv,
            device_id={name: to}, device_id_type=MESH)
        copy.start()
        return copy

    incoming, kept = [], []
    mine = pl.ds(z * per, per)
    for h in range(halves):
        arriving = []
        for d in range(nz - 1, 0, -1):
            to = peer(z, d, nz)
            arriving.append(remote(x_ref.at[to * halves + h], q[h].at[:, mine],
                                   in_s.at[h, d], in_r.at[h, d], "freq", to))
        own = pltpu.make_async_copy(x_ref.at[z * halves + h], q[h].at[:, mine], own_sem.at[h])
        own.start()
        incoming.append(arriving)
        kept.append(own)

    lane_j = lax.broadcasted_iota(jnp.int32, (nb, width), 1) // nb

    def arrive(h):
        kept[h].wait()
        for copy in incoming[h]:
            copy.wait_recv()
        weights = w_ref[:, pl.ds(pl.multiple_of((z * halves + h) * pts, pts), pts)]

        def widen(f, carry):
            for e in range(2):
                value = q[h][e, f].astype(F32)
                qf[e, f] = value
                wq[e, f] = value * weights
            return carry

        lax.fori_loop(0, freqs, widen, 0)

    def targets(h, g, p, i):
        at = [lax.rem((g + p) * per + i + j, freqs) for j in range(per)]
        return jnp.concatenate([q[h][e, t] for e in range(2) for t in at], axis=0)

    def grams(h, ch):
        def one(step, carry):
            r = step // nz
            g = step % nz
            p = partners_ref[r, g]
            for ii in range(each):
                i = ch * each + ii
                first_re = wq[0, g * per + i]
                first_im = wq[1, g * per + i]
                for j in range(per):
                    second_re = qf[0, p * per + j]
                    second_im = qf[1, p * per + j]
                    prod[pl.ds(j * nb, nb), :] = (first_re * second_re - first_im * second_im).astype(BF16)
                    prod[pl.ds(width + j * nb, nb), :] = (first_re * second_im + first_im * second_re).astype(BF16)
                full = lax.dot_general(prod[...], targets(h, g, p, i), (((1,), (1,)), ((), ())),
                                       preferred_element_type=F32)
                g_re = full[:width, :width] + full[width:, width:]
                g_im = full[:width, width:] - full[width:, :width]
                re, im = g_re[:nb], g_im[:nb]
                for j in range(1, per):
                    keep = lane_j == j
                    re = jnp.where(keep, g_re[j * nb:(j + 1) * nb], re)
                    im = jnp.where(keep, g_im[j * nb:(j + 1) * nb], im)
                both = jnp.concatenate([re, im], axis=0)
                at = pl.ds(ii * 2 * nb, 2 * nb)
                if h > 0:
                    both = both + gf[ch, r, g, at, :]
                gf[ch, r, g, at, :] = both
            return carry

        lax.fori_loop(0, rounds * nz, one, 0)

    half_at = pl.ds(pl.multiple_of(c * half, half), half)
    part_at = pl.ds(pl.multiple_of(c * half + x * part, part), part)
    flight = {}
    sent = []

    def await_all(ch, stage):
        for copy in flight[ch, stage]:
            copy.wait_recv()
        sent.extend(flight[ch, stage])

    def modes(ch, zk):
        for ii in range(each):
            i = ch * each + ii
            at = ii * 2 * nb
            totals = [None] * halves
            for r in range(rounds):
                p = partners_ref[r, zk]
                re = gfull[ch, r, zk, pl.ds(at, nb), :]
                im = gfull[ch, r, zk, pl.ds(at + nb, nb), :]
                left = jnp.concatenate([jnp.concatenate([re, -im], axis=1),
                                        jnp.concatenate([im, re], axis=1)], axis=0)
                for h in range(halves):
                    term = jnp.dot(left, targets(h, zk, p, i), preferred_element_type=F32)
                    totals[h] = term if totals[h] is None else totals[h] + term
            for h in range(halves):
                mo[zk * halves + h, pl.ds(ch * rows + at, 2 * nb), :] = (totals[h] * mode_scale).astype(BF16)

    def stage_run(ch, stage):
        out = []
        if stage == 0:
            grams(halves - 1, ch)
            for d in range(1, nc):
                to = peer(c, d, nc)
                at = pl.ds(pl.multiple_of(to * half, half), half)
                out.append(remote(gf.at[ch, :, :, at, :], r1.at[ch, d - 1], c_s.at[ch, d], c_r.at[ch, d], "blk", to))
        elif stage == 1:
            await_all(ch, 0)
            total = gf[ch, :, :, half_at, :]
            for d in range(1, nc):
                total = total + r1[ch, d - 1]
            b2[ch] = total.astype(BF16)
            gf[ch, :, :, half_at, :] = total
            for d in range(1, nx):
                to = peer(x, d, nx)
                at = pl.ds(pl.multiple_of(to * part, part), part)
                out.append(remote(b2.at[ch, :, :, at, :], r2.at[ch, d - 1], x_s.at[ch, d], x_r.at[ch, d], "space", to))
        elif stage == 2:
            await_all(ch, 1)
            total = gf[ch, :, :, part_at, :]
            for d in range(1, nx):
                total = total + r2[ch, d - 1].astype(F32)
            b3[ch] = total.astype(BF16)
            gf[ch, :, :, part_at, :] = total
            for d in range(nz - 1, 0, -1):
                to = peer(z, d, nz)
                out.append(remote(b3.at[ch, :, to], r3.at[ch, d - 1], z_s.at[ch, d], z_r.at[ch, d], "freq", to))
        elif stage == 3:
            await_all(ch, 2)
            total = gf[ch, :, z, part_at, :]
            for d in range(1, nz):
                total = total + r3[ch, d - 1].astype(F32)
            row = lax.broadcasted_iota(jnp.int32, (part, width), 0) + (c * half + x * part)
            lane = lax.broadcasted_iota(jnp.int32, (part, width), 1)
            last = jnp.maximum(lax.rem(row, nb), lax.rem(lane, nb))
            total = jnp.where((last < count_ref[0])[None], total * gram_scale, 0.0)
            gfull[ch, :, z, part_at, :] = total.astype(BF16)
            block = gfull.at[ch, :, z, part_at, :]
            for d in range(nz - 1, 0, -1):
                to = peer(z, d, nz)
                out.append(remote(block, block, gz_s.at[ch, d], gz_r.at[ch, d], "freq", to))
        elif stage == 4:
            await_all(ch, 3)
            block = gfull.at[ch, :, :, part_at, :]
            for d in range(1, nx):
                out.append(remote(block, block, gx_s.at[ch, d], gx_r.at[ch, d], "space", peer(x, d, nx)))
        elif stage == 5:
            await_all(ch, 4)
            block = gfull.at[ch, :, :, half_at, :]
            for d in range(1, nc):
                out.append(remote(block, block, gc_s.at[ch, d], gc_r.at[ch, d], "blk", peer(c, d, nc)))
        else:
            await_all(ch, 5)
            at = pl.ds(ch * rows, rows)
            for d in range(nz - 1, 0, -1):
                to = peer(z, d, nz)
                modes(ch, to)
                out.append(remote(mo.at[pl.ds(to * halves, halves), at, :],
                                  out_ref.at[pl.ds(z * halves, halves), at, :],
                                  out_s.at[ch, d], out_r.at[ch, d], "freq", to))
            modes(ch, z)
        flight[ch, stage] = out

    for h in range(halves):
        arrive(h)
        if h < halves - 1:
            for ch in range(chunks):
                grams(h, ch)
    for tick in range(7 + chunks - 1):
        for ch in range(chunks - 1, -1, -1):
            if 0 <= tick - ch < 7:
                stage_run(ch, tick - ch)

    own = pltpu.make_async_copy(mo.at[pl.ds(z * halves, halves)], out_ref.at[pl.ds(z * halves, halves)], own_sem.at[0])
    own.start()
    for ch in range(chunks):
        for r in range(rounds):
            for ii in range(each):
                for e in range(2):
                    value = gfull[ch, r, z, pl.ds((ii * 2 + e) * nb, nb), :].astype(F32)
                    for j in range(per):
                        gram_ref[r, ch * each + ii, j, e] = value[:, j * nb:(j + 1) * nb]
    own.wait()
    for ch in range(chunks):
        await_all(ch, 6)
    for copy in sum(incoming, []) + sent:
        copy.wait_send()


def body(sizes, realizations, weights, partners, block_count):
    nz, nx, nc = sizes
    per, nb, _, points = realizations.shape
    rounds = partners.shape[0]
    halves = 2 if points % (nz * 256) == 0 else 1
    pts = points // (nz * halves)
    chunks = max(1, min(per, per * 2 * nb // (nc * nx * 16)))
    fields = realizations.reshape(per, nb, 2, nz * halves, pts).transpose(3, 2, 0, 1, 4)
    width = per * nb
    rows = 2 * width // chunks
    half = rows // nc
    part = half // nx
    freqs = nz * per
    dims = (nz, nx, nc, rounds, per, nb, pts, halves, chunks,
            1.0 / math.sqrt(points * nx * nc), 1.0 / math.sqrt(rounds * per * nb))
    dma = pltpu.SemaphoreType.DMA
    vmem = pl.BlockSpec(memory_space=pltpu.VMEM)
    smem = pl.BlockSpec(memory_space=pltpu.SMEM)
    modes, grams = pl.pallas_call(
        functools.partial(kernel, dims),
        out_shape=(jax.ShapeDtypeStruct((nz * halves, 2 * width, pts), BF16),
                   jax.ShapeDtypeStruct((rounds, per, per, 2, nb, nb), F32)),
        in_specs=[smem, smem, vmem, vmem],
        out_specs=(vmem, vmem),
        scratch_shapes=[
            tuple(pltpu.VMEM((2, freqs, nb, pts), BF16) for _ in range(halves)),
            pltpu.VMEM((2, freqs, nb, pts), F32),
            pltpu.VMEM((2, freqs, nb, pts), F32),
            pltpu.VMEM((2 * width, pts), BF16),
            pltpu.VMEM((chunks, rounds, nz, rows, width), F32),
            pltpu.VMEM((chunks, nc - 1, rounds, nz, half, width), F32),
            pltpu.VMEM((chunks, rounds, nz, half, width), BF16),
            pltpu.VMEM((chunks, nx - 1, rounds, nz, part, width), BF16),
            pltpu.VMEM((chunks, rounds, nz, part, width), BF16),
            pltpu.VMEM((chunks, nz - 1, rounds, part, width), BF16),
            pltpu.VMEM((chunks, rounds, nz, rows, width), BF16),
            pltpu.VMEM((nz * halves, 2 * width, pts), BF16),
            dma((halves,)),
            dma((halves, nz)), dma((halves, nz)),
            dma((chunks, nc)), dma((chunks, nc)),
            dma((chunks, nx)), dma((chunks, nx)),
            dma((chunks, nz)), dma((chunks, nz)),
            dma((chunks, nz)), dma((chunks, nz)),
            dma((chunks, nx)), dma((chunks, nx)),
            dma((chunks, nc)), dma((chunks, nc)),
            dma((chunks, nz)), dma((chunks, nz)),
        ],
        compiler_params=pltpu.CompilerParams(
            collective_id=0, has_side_effects=True, vmem_limit_bytes=56 * 1024 * 1024),
    )(partners, block_count, fields, weights.reshape(1, points))
    modes = modes.reshape(nz * halves, per, 2, nb, pts).transpose(1, 3, 2, 0, 4).reshape(per, nb, 2, points)
    return (modes, grams)


def solution(mesh):
    placed = (
        P("freq", "groups", None, ("space", "blk")),
        P(("groups", "space", "blk")),
        P(),
        P("groups"),
    )
    return jax.shard_map(
        functools.partial(body, tuple(mesh.shape[a] for a in AXES)),
        mesh=mesh,
        in_specs=placed,
        out_specs=(
            P("freq", "groups", None, ("space", "blk")),
            P("groups", "freq", None, None, None, None),
        ),
        check_vma=False,
    )
```

```python
import functools
import math

import jax
import jax.numpy as jnp
from jax import lax
from jax.experimental import pallas as pl
from jax.experimental.pallas import tpu as pltpu
from jax.sharding import PartitionSpec as P

MESH = pl.DeviceIdType.MESH
F32 = jnp.float32
BF16 = jnp.bfloat16
AXES = ("freq", "space", "blk")


def kernel(dims, partners_ref, count_ref, x_ref, w_ref, out_ref, gram_ref,
           q, qf, wq, gf, r1, b2, r2, b3, r3, gfull, mo,
           own_sem, in_s, in_r, c_s, c_r, x_s, x_r, z_s, z_r,
           gz_s, gz_r, gx_s, gx_r, gc_s, gc_r, out_s, out_r):
    nz, nx, nc, rounds, per, nb, pts, halves, chunks, gram_scale, mode_scale = dims
    width = per * nb
    each = per // chunks
    rows = each * 2 * nb
    half = rows // nc
    part = half // nx
    freqs = nz * per
    z = lax.axis_index("freq")
    x = lax.axis_index("space")
    c = lax.axis_index("blk")

    def peer(me, d, n):
        return lax.rem(me + d, n)

    barrier = pltpu.get_barrier_semaphore()
    for name, me, n in (("freq", z, nz), ("space", x, nx), ("blk", c, nc)):
        for d in range(1, n):
            pl.semaphore_signal(barrier, inc=1, device_id={name: peer(me, d, n)}, device_id_type=MESH)
    pl.semaphore_wait(barrier, nz + nx + nc - 3)

    def remote(src, dst, send, recv, name, to):
        copy = pltpu.make_async_remote_copy(
            src_ref=src, dst_ref=dst, send_sem=send, recv_sem=recv,
            device_id={name: to}, device_id_type=MESH)
        copy.start()
        return copy

    incoming, kept = [], []
    mine = pl.ds(z * per, per)
    for h in range(halves):
        arriving = []
        for d in range(nz - 1, 0, -1):
            to = peer(z, d, nz)
            arriving.append(remote(x_ref.at[to * halves + h], q[h].at[:, mine],
                                   in_s.at[h, d], in_r.at[h, d], "freq", to))
        own = pltpu.make_async_copy(x_ref.at[z * halves + h], q[h].at[:, mine], own_sem.at[h])
        own.start()
        incoming.append(arriving)
        kept.append(own)

    lane_j = lax.broadcasted_iota(jnp.int32, (nb, width), 1) // nb

    def arrive(h):
        kept[h].wait()
        for copy in incoming[h]:
            copy.wait_recv()
        weights = w_ref[:, pl.ds(pl.multiple_of((z * halves + h) * pts, pts), pts)]

        def widen(f, carry):
            for e in range(2):
                value = q[h][e, f].astype(F32)
                qf[e, f] = value
                wq[e, f] = value * weights
            return carry

        lax.fori_loop(0, freqs, widen, 0)

    def targets(h, g, p, i):
        at = [lax.rem((g + p) * per + i + j, freqs) for j in range(per)]
        return jnp.concatenate([q[h][e, t] for e in range(2) for t in at], axis=0)

    def grams(h, ch):
        def one(g, carry):
            for r in range(rounds):
                p = partners_ref[r, g]
                for ii in range(each):
                    i = ch * each + ii
                    first_re = wq[0, g * per + i]
                    first_im = wq[1, g * per + i]
                    reals, imags = [], []
                    for j in range(per):
                        second_re = qf[0, p * per + j]
                        second_im = qf[1, p * per + j]
                        reals.append((first_re * second_re - first_im * second_im).astype(BF16))
                        imags.append((first_re * second_im + first_im * second_re).astype(BF16))
                    full = lax.dot_general(jnp.concatenate(reals + imags, axis=0), targets(h, g, p, i),
                                           (((1,), (1,)), ((), ())), preferred_element_type=F32)
                    g_re = full[:width, :width] + full[width:, width:]
                    g_im = full[:width, width:] - full[width:, :width]
                    re, im = g_re[:nb], g_im[:nb]
                    for j in range(1, per):
                        keep = lane_j == j
                        re = jnp.where(keep, g_re[j * nb:(j + 1) * nb], re)
                        im = jnp.where(keep, g_im[j * nb:(j + 1) * nb], im)
                    both = jnp.concatenate([re, im], axis=0)
                    at = pl.ds(ii * 2 * nb, 2 * nb)
                    if h > 0:
                        both = both + gf[ch, r, g, at, :]
                    gf[ch, r, g, at, :] = both
            return carry

        lax.fori_loop(0, nz, one, 0)

    half_at = pl.ds(pl.multiple_of(c * half, half), half)
    part_at = pl.ds(pl.multiple_of(c * half + x * part, part), part)
    flight = {}
    sent = []

    def await_all(ch, stage):
        for copy in flight[ch, stage]:
            copy.wait_recv()
        sent.extend(flight[ch, stage])

    def modes(ch, zk):
        for ii in range(each):
            i = ch * each + ii
            at = ii * 2 * nb
            totals = [None] * halves
            for r in range(rounds):
                p = partners_ref[r, zk]
                re = gfull[ch, r, zk, pl.ds(at, nb), :]
                im = gfull[ch, r, zk, pl.ds(at + nb, nb), :]
                left = jnp.concatenate([jnp.concatenate([re, -im], axis=1),
                                        jnp.concatenate([im, re], axis=1)], axis=0)
                for h in range(halves):
                    term = jnp.dot(left, targets(h, zk, p, i), preferred_element_type=F32)
                    totals[h] = term if totals[h] is None else totals[h] + term
            for h in range(halves):
                mo[zk * halves + h, pl.ds(ch * rows + at, 2 * nb), :] = (totals[h] * mode_scale).astype(BF16)

    def stage_run(ch, stage):
        out = []
        if stage == 0:
            grams(halves - 1, ch)
            for d in range(1, nc):
                to = peer(c, d, nc)
                at = pl.ds(pl.multiple_of(to * half, half), half)
                out.append(remote(gf.at[ch, :, :, at, :], r1.at[ch, d - 1], c_s.at[ch, d], c_r.at[ch, d], "blk", to))
        elif stage == 1:
            await_all(ch, 0)
            total = gf[ch, :, :, half_at, :]
            for d in range(1, nc):
                total = total + r1[ch, d - 1]
            b2[ch] = total.astype(BF16)
            gf[ch, :, :, half_at, :] = total
            for d in range(1, nx):
                to = peer(x, d, nx)
                at = pl.ds(pl.multiple_of(to * part, part), part)
                out.append(remote(b2.at[ch, :, :, at, :], r2.at[ch, d - 1], x_s.at[ch, d], x_r.at[ch, d], "space", to))
        elif stage == 2:
            await_all(ch, 1)
            total = gf[ch, :, :, part_at, :]
            for d in range(1, nx):
                total = total + r2[ch, d - 1].astype(F32)
            b3[ch] = total.astype(BF16)
            gf[ch, :, :, part_at, :] = total
            for d in range(nz - 1, 0, -1):
                to = peer(z, d, nz)
                out.append(remote(b3.at[ch, :, to], r3.at[ch, d - 1], z_s.at[ch, d], z_r.at[ch, d], "freq", to))
        elif stage == 3:
            await_all(ch, 2)
            total = gf[ch, :, z, part_at, :]
            for d in range(1, nz):
                total = total + r3[ch, d - 1].astype(F32)
            row = lax.broadcasted_iota(jnp.int32, (part, width), 0) + (c * half + x * part)
            lane = lax.broadcasted_iota(jnp.int32, (part, width), 1)
            last = jnp.maximum(lax.rem(row, nb), lax.rem(lane, nb))
            total = jnp.where((last < count_ref[0])[None], total * gram_scale, 0.0)
            gfull[ch, :, z, part_at, :] = total.astype(BF16)
            block = gfull.at[ch, :, z, part_at, :]
            for d in range(nz - 1, 0, -1):
                to = peer(z, d, nz)
                out.append(remote(block, block, gz_s.at[ch, d], gz_r.at[ch, d], "freq", to))
        elif stage == 4:
            await_all(ch, 3)
            block = gfull.at[ch, :, :, part_at, :]
            for d in range(1, nx):
                out.append(remote(block, block, gx_s.at[ch, d], gx_r.at[ch, d], "space", peer(x, d, nx)))
        elif stage == 5:
            await_all(ch, 4)
            block = gfull.at[ch, :, :, half_at, :]
            for d in range(1, nc):
                out.append(remote(block, block, gc_s.at[ch, d], gc_r.at[ch, d], "blk", peer(c, d, nc)))
        else:
            await_all(ch, 5)
            at = pl.ds(ch * rows, rows)
            for d in range(nz - 1, 0, -1):
                to = peer(z, d, nz)
                modes(ch, to)
                out.append(remote(mo.at[pl.ds(to * halves, halves), at, :],
                                  out_ref.at[pl.ds(z * halves, halves), at, :],
                                  out_s.at[ch, d], out_r.at[ch, d], "freq", to))
            modes(ch, z)
        flight[ch, stage] = out

    for h in range(halves):
        arrive(h)
        if h < halves - 1:
            for ch in range(chunks):
                grams(h, ch)
    for tick in range(7 + chunks - 1):
        for ch in range(chunks - 1, -1, -1):
            if 0 <= tick - ch < 7:
                stage_run(ch, tick - ch)

    own = pltpu.make_async_copy(mo.at[pl.ds(z * halves, halves)], out_ref.at[pl.ds(z * halves, halves)], own_sem.at[0])
    own.start()
    for ch in range(chunks):
        for r in range(rounds):
            for ii in range(each):
                for e in range(2):
                    value = gfull[ch, r, z, pl.ds((ii * 2 + e) * nb, nb), :].astype(F32)
                    for j in range(per):
                        gram_ref[r, ch * each + ii, j, e] = value[:, j * nb:(j + 1) * nb]
    own.wait()
    for ch in range(chunks):
        await_all(ch, 6)
    for copy in sum(incoming, []) + sent:
        copy.wait_send()


def body(sizes, realizations, weights, partners, block_count):
    nz, nx, nc = sizes
    per, nb, _, points = realizations.shape
    rounds = partners.shape[0]
    halves = 2 if points % (nz * 256) == 0 else 1
    pts = points // (nz * halves)
    chunks = max(1, min(per, per * 2 * nb // (nc * nx * 16)))
    fields = realizations.reshape(per, nb, 2, nz * halves, pts).transpose(3, 2, 0, 1, 4)
    width = per * nb
    rows = 2 * width // chunks
    half = rows // nc
    part = half // nx
    freqs = nz * per
    dims = (nz, nx, nc, rounds, per, nb, pts, halves, chunks,
            1.0 / math.sqrt(points * nx * nc), 1.0 / math.sqrt(rounds * per * nb))
    dma = pltpu.SemaphoreType.DMA
    vmem = pl.BlockSpec(memory_space=pltpu.VMEM)
    smem = pl.BlockSpec(memory_space=pltpu.SMEM)
    modes, grams = pl.pallas_call(
        functools.partial(kernel, dims),
        out_shape=(jax.ShapeDtypeStruct((nz * halves, 2 * width, pts), BF16),
                   jax.ShapeDtypeStruct((rounds, per, per, 2, nb, nb), F32)),
        in_specs=[smem, smem, vmem, vmem],
        out_specs=(vmem, vmem),
        scratch_shapes=[
            tuple(pltpu.VMEM((2, freqs, nb, pts), BF16) for _ in range(halves)),
            pltpu.VMEM((2, freqs, nb, pts), F32),
            pltpu.VMEM((2, freqs, nb, pts), F32),
            pltpu.VMEM((chunks, rounds, nz, rows, width), F32),
            pltpu.VMEM((chunks, nc - 1, rounds, nz, half, width), F32),
            pltpu.VMEM((chunks, rounds, nz, half, width), BF16),
            pltpu.VMEM((chunks, nx - 1, rounds, nz, part, width), BF16),
            pltpu.VMEM((chunks, rounds, nz, part, width), BF16),
            pltpu.VMEM((chunks, nz - 1, rounds, part, width), BF16),
            pltpu.VMEM((chunks, rounds, nz, rows, width), BF16),
            pltpu.VMEM((nz * halves, 2 * width, pts), BF16),
            dma((halves,)),
            dma((halves, nz)), dma((halves, nz)),
            dma((chunks, nc)), dma((chunks, nc)),
            dma((chunks, nx)), dma((chunks, nx)),
            dma((chunks, nz)), dma((chunks, nz)),
            dma((chunks, nz)), dma((chunks, nz)),
            dma((chunks, nx)), dma((chunks, nx)),
            dma((chunks, nc)), dma((chunks, nc)),
            dma((chunks, nz)), dma((chunks, nz)),
        ],
        compiler_params=pltpu.CompilerParams(
            collective_id=0, has_side_effects=True, vmem_limit_bytes=56 * 1024 * 1024),
    )(partners, block_count, fields, weights.reshape(1, points))
    modes = modes.reshape(nz * halves, per, 2, nb, pts).transpose(1, 3, 2, 0, 4).reshape(per, nb, 2, points)
    return (modes, grams)


def solution(mesh):
    placed = (
        P("freq", "groups", None, ("space", "blk")),
        P(("groups", "space", "blk")),
        P(),
        P("groups"),
    )
    return jax.shard_map(
        functools.partial(body, tuple(mesh.shape[a] for a in AXES)),
        mesh=mesh,
        in_specs=placed,
        out_specs=(
            P("freq", "groups", None, ("space", "blk")),
            P("groups", "freq", None, None, None, None),
        ),
        check_vma=False,
    )
```
